32 devices in a mesh: grp: 2 (over x), smp: 16 (over z, y, core).
Axes of the slice: x: 2, y: 2, z: 4, core: 2. Of those that a mesh axis runs over, the one named last changes fastest.
Arguments:
- dosage: bfloat16 [2048, 4096], P('smp', 'grp'), parts along dimension 1, may hold values from 0.008 to 4.5, as said below
- flags: int32 [256], P('grp'), parts along dimension 0, may hold values from 0 to 2047, as said below
- events: int32 [2048, 32], P('smp', 'grp'), parts along dimension 1, may hold values from 0 to 1, as said below
- offsets: float32 [2048, 32], P('smp', 'grp'), parts along dimension 1, may hold values from -3 to 3
Outputs:
- effect: float32 [16, 256], P(None, 'grp'), parts along dimension 1
- zscore: float32 [16, 256], P(None, 'grp'), parts along dimension 1
The draws below stay inside these ranges and needn't reach their ends.
There are 2 independent parts, one for each index of `grp`. The reference program is written for one: setup_inputs(seed, part) draws one part's arguments, and reference() takes and returns one part's arrays. A program takes and returns all parts, laid end to end along the dimension named above; each array names one. Nothing has to cross between parts.
Inputs may be any that keep to these rules, and one draw needn't show every extreme that they name: `flags`: 128 distinct column numbers in rising order, the first 0 and the last 2047. `events`: 0 or 1; every endpoint has an event at the first sample. `dosage`: positive dosages.
All inputs are finite; a program needn't handle non-finite values.
Results may differ from the reference program's by a relative error of at most 0.0013.
Values sent between devices are 32-bit elements; how exact they have to be, the bound alone decides.
A program may use at most 64 MiB of HBM per device.

```python
import jax
import jax.numpy as jnp
from jax import lax

E = 16
V = 128
C = 2048
ITERS = 3
N = 2048


def draw_flags(key, part):
    middle = jax.random.permutation(key, jnp.arange(1, C - 1, dtype=jnp.int32))[:V - 2]
    chosen = jnp.concatenate([jnp.zeros((1,), jnp.int32), middle.astype(jnp.int32), jnp.full((1,), C - 1, jnp.int32)])
    return jnp.sort(chosen).astype(jnp.int32)


def event_table(key):
    picks = jax.random.randint(jax.random.fold_in(key, 11), (N, E), 0, 16)
    marked = (picks == 0).astype(jnp.int32)
    first_row = (jnp.arange(N, dtype=jnp.int32) == 0).astype(jnp.int32)[:, None]
    return jnp.maximum(marked, first_row).astype(jnp.int32)


def draw_events(key, part):
    return event_table(key)


def draw_dosage(key, part):
    marked = event_table(key).astype(jnp.float32)
    key_base = jax.random.fold_in(key, 21)
    key_link = jax.random.fold_in(key, 22)
    key_sign = jax.random.fold_in(key, 23)
    key_level = jax.random.fold_in(key, 24)
    base = jnp.exp(jax.random.uniform(key_base, (N, C), jnp.float32, jnp.log(0.02), jnp.log(2.0)))
    linked = jax.random.randint(key_link, (C,), 0, E)
    signs = (2 * jax.random.randint(key_sign, (C,), 0, 2) - 1).astype(jnp.float32)
    strength = jax.random.uniform(key_level, (C,), jnp.float32, 0.3, 0.8) * signs
    chosen = jnp.take(marked, linked, axis=1)
    return (base * jnp.exp(strength[None, :] * chosen)).astype(jnp.bfloat16)


def shard_levels(stream_key, extent, cuts, smallest, largest):
    level = 1.0
    for axis_at, parts in cuts:
        steps = jax.random.uniform(jax.random.fold_in(jax.random.fold_in(stream_key, 6), axis_at), (parts,), jnp.float32, smallest / len(cuts), largest / len(cuts))
        level = level * jnp.repeat(jnp.exp(steps), extent[axis_at] // parts).reshape((-1,) + (1,) * (len(extent) - 1 - axis_at))
    return level


def scatter_about(stream_key, shape, spread, limit, shards=(), kind=jnp.bfloat16):
    drawn = spread * jax.random.normal(stream_key, shape, jnp.float32)
    if shards:
        drawn = drawn * shard_levels(stream_key, shape, shards, -0.22, 0.18)
    return jnp.clip(drawn, -limit, limit).astype(kind)


def setup_inputs(seed: int = 0, part: int = 0) -> dict:
    splits = jax.random.split(jax.random.key(seed), 5)
    part_keys = jax.random.split(jax.random.fold_in(splits[4], part), 5)
    return {
        "dosage": draw_dosage(jax.random.fold_in(jax.random.fold_in(splits[4], part), 71), part),
        "flags": draw_flags(jax.random.fold_in(jax.random.fold_in(splits[4], part), 71), part),
        "events": draw_events(jax.random.fold_in(jax.random.fold_in(splits[4], part), 71), part),
        "offsets": scatter_about(part_keys[3], (N, E), 0.5, 3.0, ((0, 16),), jnp.float32),
    }


def reference(dosage, flags, events, offsets):
    genotype = jnp.take(dosage, flags, axis=1).astype(jnp.float32)

    def fit_endpoint(inputs):
        hazard_offset, indicator = inputs
        effect = jnp.zeros((genotype.shape[1],), jnp.float32)
        zscore = effect
        dose = genotype
        for sweep in range(ITERS):
            weight = jnp.exp(hazard_offset[:, None] + effect[None, :] * dose)
            moments = jnp.stack([weight, weight * dose, weight * dose * dose, weight * dose * dose * dose])
            suffix = lax.cumsum(moments, axis=1, reverse=True)
            first = suffix[1] / suffix[0]
            second = suffix[2] / suffix[0]
            third = suffix[3] / suffix[0]
            mark = indicator[:, None]
            score = lax.optimization_barrier(jnp.sum(mark * (dose - first), axis=0))
            information = lax.optimization_barrier(jnp.sum(mark * (second - first * first), axis=0))
            skewness = lax.optimization_barrier(jnp.sum(mark * (third - 3.0 * first * second + 2.0 * first * first * first), axis=0))
            effect = effect + (score + 0.5 * skewness / information) / information
            zscore = effect * jnp.sqrt(information)
        return (effect, zscore)
    effect, zscore = lax.map(fit_endpoint, (offsets.T, events.T.astype(jnp.float32)))
    return (effect, zscore)
```

```python
import functools

import jax
import jax.numpy as jnp
from jax import lax
from jax.experimental import pallas as pl
from jax.experimental.pallas import tpu as pltpu
from jax.sharding import PartitionSpec as P

ITERS = 3
SUB = 8
LIMIT = 48 * 2**20
GROUP = 3
LOG2E = 1.4426950408889634
MESH = pl.DeviceIdType.MESH
F32 = jnp.float32
BF16 = jnp.bfloat16


def thirds(x):
    high = x.astype(BF16).astype(F32)
    rest = x - high
    middle = rest.astype(BF16).astype(F32)
    return high, middle, rest - middle


def transposed_dot(a, b):
    return lax.dot_general(a, b, (((0,), (0,)), ((), ())), preferred_element_type=F32)


def iota(shape, dim):
    return lax.broadcasted_iota(jnp.int32, shape, dim)


def kernel(
    n, flags_hbm, dosage_hbm, offsets_hbm, events_hbm, held,
    flags_ref, dosage_ref, offsets_ref, events_ref,
    send, recv, dose_ref, shift_ref, mark_ref, sums_ref, even_ref, odd_ref, rsend,
    load_sem, send_sem, recv_sem, rsend_sem, rrecv_sem,
):
    me = lax.axis_index("smp")
    rows, columns = dosage_ref.shape
    endpoints = offsets_ref.shape[0]
    part = endpoints // 2
    variants = flags_ref.shape[1]
    own = variants * 2 // n
    lanes = dose_ref.shape[1]
    steps = rows // SUB
    low = lax.convert_element_type(me < n // 2, jnp.int32)

    def far(at):
        up = at + lax.convert_element_type(at >= me, jnp.int32)
        down = n - 1 - at
        down = down - lax.convert_element_type(down <= me, jnp.int32)
        return low * down + (1 - low) * up

    loads = [
        pltpu.make_async_copy(src, dst, load_sem.at[at])
        for at, (src, dst) in enumerate(
            ((flags_hbm, flags_ref), (dosage_hbm, dosage_ref), (offsets_hbm, offsets_ref), (events_hbm, events_ref))
        )
    ]
    for load in loads:
        load.start()

    barrier = pltpu.get_barrier_semaphore()
    for at in range(n - 1):
        pl.semaphore_signal(barrier, inc=1, device_id={"smp": far(at)}, device_id_type=MESH)

    line = iota((rows, rows), 1)
    order = (iota((rows, rows), 0) == lax.rem(line, SUB) * steps + lax.div(line, SUB)).astype(F32).astype(BF16)

    loads[2].wait()
    loads[3].wait()
    four = jnp.concatenate([*thirds(offsets_ref[...] * LOG2E), events_ref[...].astype(F32)], axis=0)
    four = jnp.dot(four.astype(BF16), order, preferred_element_type=F32)
    high, middle, low_part, events = (four[k * endpoints : (k + 1) * endpoints] for k in range(4))
    offsets = (high + middle) + low_part
    for k in range(n):
        for at, values in ((own, offsets), (own + part, events)):
            send[k, pl.ds(at, part), :] = values[k % 2 * part : (k % 2 + 1) * part]

    loads[0].wait()
    chosen = (iota((columns, variants), 0) == flags_ref[...]).astype(F32).astype(BF16)
    loads[1].wait()
    genotype = jnp.dot(dosage_ref[...], chosen, preferred_element_type=F32).astype(BF16)
    genotype = transposed_dot(genotype, order)
    for k in range(n):
        send[k, pl.ds(0, own), :] = genotype[k // 2 * own : (k // 2 + 1) * own]

    pl.semaphore_wait(barrier, n - 1)

    def copy(at, slot):
        return pltpu.make_async_remote_copy(
            src_ref=send.at[at], dst_ref=recv.at[slot], send_sem=send_sem.at[0], recv_sem=recv_sem.at[slot],
            device_id={"smp": at}, device_id_type=MESH,
        )

    def rcopy(at):
        return pltpu.make_async_remote_copy(
            src_ref=rsend, dst_ref=held.at[me], send_sem=rsend_sem.at[0], recv_sem=rrecv_sem.at[0],
            device_id={"smp": at}, device_id_type=MESH,
        )

    for at in range(n - 1):
        copy(far(at), me).start()

    lane_e = iota((part, lanes), 1)
    lane_v = iota((own, lanes), 1)
    spread_e = (lax.div(lane_e, own) == iota((part, lanes), 0)).astype(F32)
    spread_v = jnp.logical_and(lax.rem(lane_v, own) == iota((own, lanes), 0), lane_v < own * part).astype(F32)
    none_e, none_v = jnp.zeros_like(spread_e), jnp.zeros_like(spread_v)
    spread = jnp.concatenate(
        [jnp.concatenate([none_v, none_v, spread_v], axis=1)]
        + [jnp.concatenate([spread_e, none_e, none_e], axis=1)] * 3
        + [jnp.concatenate([none_e, spread_e, none_e], axis=1)],
        axis=0,
    ).astype(BF16)

    def tile(block, t):
        return pl.ds(pl.multiple_of(block * rows + t * SUB, SUB), SUB)

    def moments(weight, dose, total, into, base):
        for k in range(4):
            total[k] = total[k] + weight
            into[base, pl.ds(k * lanes, lanes)] = total[k]
            if k < 3:
                weight = weight * dose

    zero = jnp.zeros((SUB, lanes), F32)

    def expand(slots, pieces, marked):
        mixed = []
        for values in pieces:
            doses, samples, events = values[:own], values[own : own + part], values[own + part :]
            tall = jnp.concatenate([doses, *thirds(samples), events], axis=0)
            mixed.append(transposed_dot(tall.astype(BF16), spread))
        for slot, values in zip(slots, mixed):
            total = [zero] * 4
            for t in reversed(range(steps)):
                shift, mark, dose = (values[t * SUB : (t + 1) * SUB, k * lanes : (k + 1) * lanes] for k in range(3))
                at = tile(slot, t)
                shift_ref[at, :] = shift
                mark_ref[at, :] = mark
                dose_ref[at, :] = dose
                marked = marked + mark * dose
                moments(jnp.exp2(shift), dose, total, sums_ref, at)
        return marked

    group = max(size for size in range(1, GROUP + 1) if (n - 1) % size == 0)

    def arrive(step, marked):
        slots = [far(n - 2 - (step * group + at)) for at in range(group)]
        for slot in slots:
            copy(slot, slot).wait_recv()
        return expand(slots, [recv[slot] for slot in slots], marked)

    marked = expand([me], [send[me]], zero)
    marked = lax.fori_loop(0, (n - 1) // group, arrive, marked)

    below = iota((SUB, lanes), 0)

    def scan(total, later):
        carry, fresh = [], []
        for x, run in zip(total, later):
            e = jnp.where(below < SUB - 1, pltpu.roll(x, SUB - 1, 0), 0.0)
            for shift in (1, 2, 4):
                e = e + jnp.where(below < SUB - shift, pltpu.roll(e, SUB - shift, 0), 0.0)
            carry.append(e + run)
            fresh.append(run + jnp.broadcast_to((x + e)[0:1], (SUB, lanes)))
        return carry, fresh

    def add_moments(block, slope, into):
        total = [zero] * 4
        for t in reversed(range(steps)):
            at = tile(block, t)
            dose = dose_ref[at, :]
            moments(jnp.exp2(shift_ref[at, :] + slope * dose), dose, total, into, pl.ds(t * SUB, SUB))
        return total

    def add_terms(block, source, base, carry, sums):
        first_sum, information, skewness = sums
        for t in reversed(range(steps)):
            here = pl.ds(base + t * SUB, SUB) if isinstance(base, int) else tile(base, t)
            s0, s1, s2, s3 = (source[here, pl.ds(k * lanes, lanes)] + carry[k] for k in range(4))
            mark = mark_ref[tile(block, t), :]
            inverse = 1.0 / s0
            scaled = mark * inverse
            first = s1 * inverse
            one = mark * first
            two = s2 * scaled
            spread = two - one * first
            first_sum = first_sum + one
            information = information + spread
            skewness = skewness + (s3 * scaled - first * (two + (spread + spread)))
        return first_sum, information, skewness

    def finish(effect, sums):
        first_sum, information, skewness = sums
        score, information, skewness = (
            jnp.sum(x, axis=0, keepdims=True) for x in (marked - first_sum, information, skewness)
        )
        effect = effect + (score + 0.5 * skewness / information) / information
        return effect, effect * jnp.sqrt(information)

    zeros = (zero,) * 3

    def opening(at, state):
        later, sums = state
        block = n - 1 - at
        total = [sums_ref[tile(block, 0), pl.ds(k * lanes, lanes)] for k in range(4)]
        carry, later = scan(total, later)
        return tuple(later), add_terms(block, sums_ref, block, carry, sums)

    _, sums = lax.fori_loop(0, n, opening, ((zero,) * 4, zeros), unroll=2)
    effect, zscore = finish(jnp.zeros((1, lanes), F32), sums)

    def sweep(_, state):
        effect, _ = state
        slope = jnp.broadcast_to(effect * LOG2E, (SUB, lanes))
        carry, later = scan(add_moments(n - 1, slope, even_ref), [zero] * 4)

        def pair(at, state):
            carry, later, sums = state
            block = n - 1 - 2 * at
            total = add_moments(block - 1, slope, odd_ref)
            sums = add_terms(block, even_ref, 0, carry, sums)
            carry, later = scan(total, later)
            total = add_moments(block - 2, slope, even_ref)
            sums = add_terms(block - 1, odd_ref, 0, carry, sums)
            carry, later = scan(total, later)
            return tuple(carry), tuple(later), sums

        carry, later, sums = lax.fori_loop(0, n // 2 - 1, pair, (tuple(carry), tuple(later), zeros))
        total = add_moments(0, slope, odd_ref)
        sums = add_terms(1, even_ref, 0, carry, sums)
        carry, _ = scan(total, later)
        return finish(effect, add_terms(0, odd_ref, 0, carry, sums))

    effect, zscore = lax.fori_loop(0, ITERS - 1, sweep, (effect, zscore))

    rsend[0:1, :] = effect
    rsend[1:2, :] = zscore

    for at in range(n - 1):
        rcopy(far(at)).start()

    mine = pltpu.make_async_copy(rsend, held.at[me], load_sem.at[0])
    mine.start()
    pltpu.make_async_copy(send.at[pl.ds(0, n - 1)], recv.at[pl.ds(0, n - 1)], send_sem.at[0]).wait()
    mine.wait()
    whole = held.at[pl.ds(0, n - 1)]
    pltpu.make_async_copy(whole, whole, rrecv_sem.at[0]).wait()
    pltpu.make_async_copy(whole, whole, rsend_sem.at[0]).wait()


def unfold(n, held, effect_ref, zscore_ref):
    endpoints, variants = effect_ref.shape
    part = endpoints // 2
    own = variants * 2 // n
    lanes = held.shape[2]
    owner = lax.div(iota((part, lanes), 1), own) == iota((part, lanes), 0)
    fold = jnp.logical_and(
        lax.rem(iota((lanes, variants), 0), own) == lax.rem(iota((lanes, variants), 1), own),
        iota((lanes, variants), 0) < own * part,
    ).astype(F32).astype(BF16)
    column = lax.div(iota((endpoints, variants), 1), own)
    for which, out in enumerate((effect_ref, zscore_ref)):
        tall = jnp.concatenate([jnp.where(owner, held[k, which : which + 1, :], 0.0) for k in range(n)], axis=0)
        parts = [jnp.dot(third.astype(BF16), fold, preferred_element_type=F32) for third in thirds(tall)]
        tall = (parts[0] + parts[1]) + parts[2]
        result = jnp.zeros((endpoints, variants), F32)
        for c in range(n // 2):
            result = jnp.where(column == c, tall[c * endpoints : (c + 1) * endpoints], result)
        out[...] = result


def solution(mesh):
    n = mesh.shape["smp"]

    def body(dosage, flags, events, offsets):
        rows, columns = dosage.shape
        endpoints = offsets.shape[1]
        variants = flags.shape[0]
        own = variants * 2 // n
        part = endpoints // 2
        lanes = -(-own * part // 128) * 128
        out = jax.ShapeDtypeStruct((endpoints, variants), F32)
        held = pl.pallas_call(
            functools.partial(kernel, n),
            out_shape=jax.ShapeDtypeStruct((n, 2, lanes), F32),
            in_specs=[pl.BlockSpec(memory_space=pl.ANY)] * 4,
            out_specs=pl.BlockSpec(memory_space=pl.ANY),
            scratch_shapes=[
                pltpu.VMEM((1, variants), jnp.int32),
                pltpu.VMEM((rows, columns), BF16),
                pltpu.VMEM((endpoints, rows), F32),
                pltpu.VMEM((endpoints, rows), jnp.int32),
                pltpu.VMEM((n, own + 2 * part, rows), F32),
                pltpu.VMEM((n, own + 2 * part, rows), F32),
                pltpu.VMEM((n * rows, lanes), F32),
                pltpu.VMEM((n * rows, lanes), F32),
                pltpu.VMEM((n * rows, lanes), F32),
                pltpu.VMEM((n * rows, 4 * lanes), F32),
                pltpu.VMEM((rows, 4 * lanes), F32),
                pltpu.VMEM((rows, 4 * lanes), F32),
                pltpu.VMEM((2, lanes), F32),
                pltpu.SemaphoreType.DMA((4,)),
                pltpu.SemaphoreType.DMA((1,)),
                pltpu.SemaphoreType.DMA((n,)),
                pltpu.SemaphoreType.DMA((1,)),
                pltpu.SemaphoreType.DMA((1,)),
            ],
            compiler_params=pltpu.CompilerParams(collective_id=0, has_side_effects=True, vmem_limit_bytes=LIMIT),
        )(*(pltpu.with_memory_space_constraint(x, pltpu.HBM) for x in (flags.reshape(1, variants), dosage, offsets.T, events.T)))
        return pl.pallas_call(
            functools.partial(unfold, n),
            out_shape=(out, out),
            in_specs=[pl.BlockSpec(memory_space=pltpu.VMEM)],
            out_specs=[pl.BlockSpec(memory_space=pltpu.VMEM)] * 2,
            compiler_params=pltpu.CompilerParams(vmem_limit_bytes=LIMIT // 8),
        )(held)

    return jax.shard_map(
        body,
        mesh=mesh,
        in_specs=(P("smp", "grp"), P("grp"), P("smp", "grp"), P("smp", "grp")),
        out_specs=(P(None, "grp"), P(None, "grp")),
        check_vma=False,
    )
```

```python
import functools
import math

import jax
import jax.numpy as jnp
from jax import lax
from jax.experimental import pallas as pl
from jax.experimental.pallas import tpu as pltpu
from jax.sharding import PartitionSpec as P

ITERS = 3
SUB = 8
LIMIT = 48 * 2**20
LOG2E = 1.4426950408889634
MESH = pl.DeviceIdType.MESH
F32 = jnp.float32
BF16 = jnp.bfloat16


def thirds(x):
    high = x.astype(BF16).astype(F32)
    rest = x - high
    middle = rest.astype(BF16).astype(F32)
    return high, middle, rest - middle


def transposed_dot(a, b):
    return lax.dot_general(a, b, (((0,), (0,)), ((), ())), preferred_element_type=F32)


def iota(shape, dim):
    return lax.broadcasted_iota(jnp.int32, shape, dim)


def kernel(
    n, flags_hbm, dosage_hbm, offsets_hbm, events_hbm, held,
    flags_ref, dosage_ref, offsets_ref, events_ref,
    send, recv, dose_ref, shift_ref, mark_ref, sums_ref, even_ref, odd_ref, state_ref, rsend,
    load_sem, send_sem, recv_sem, rsend_sem, rrecv_sem, up,
):
    me = lax.axis_index("smp")
    rows, columns = dosage_ref.shape
    endpoints = offsets_ref.shape[0]
    part = endpoints // 2
    variants = flags_ref.shape[1]
    own = variants * 2 // n
    lanes = dose_ref.shape[1]
    steps = rows // SUB
    size = math.isqrt(n)
    planes = n // size
    plane, spot = lax.div(me, size), lax.rem(me, size)
    final = plane == planes - 1

    def others(at):
        return at + lax.convert_element_type(at >= me, jnp.int32)

    loads = [
        pltpu.make_async_copy(src, dst, load_sem.at[at])
        for at, (src, dst) in enumerate(
            ((flags_hbm, flags_ref), (dosage_hbm, dosage_ref), (offsets_hbm, offsets_ref), (events_hbm, events_ref))
        )
    ]
    for load in loads:
        load.start()

    barrier = pltpu.get_barrier_semaphore()

    def member(plane, at):
        return plane * size + lax.rem(spot + at, size)

    def signal(sem, at):
        pl.semaphore_signal(sem, inc=1, device_id={"smp": at}, device_id_type=MESH)

    @pl.when(final)
    def _():
        for at in range(1, size):
            signal(barrier, member(plane, at))

    @pl.when(jnp.logical_not(final))
    def _():
        for at in range(n - 1):
            signal(barrier, others(n - 2 - at))

    def meet():
        pl.semaphore_wait(barrier, n - 1)
        for at in range(n - size):
            signal(up.at[0], at)

    @pl.when(jnp.logical_and(final, spot >= size // 2))
    def _():
        meet()

    line = iota((rows, rows), 1)
    order = (iota((rows, rows), 0) == lax.rem(line, SUB) * steps + lax.div(line, SUB)).astype(F32).astype(BF16)

    loads[2].wait()
    loads[3].wait()
    four = jnp.concatenate([*thirds(offsets_ref[...] * LOG2E), events_ref[...].astype(F32)], axis=0)
    four = jnp.dot(four.astype(BF16), order, preferred_element_type=F32)
    high, middle, low_part, events = (four[k * endpoints : (k + 1) * endpoints] for k in range(4))
    offsets = (high + middle) + low_part
    for k in range(n):
        for at, values in ((own, offsets), (own + part, events)):
            send[k, pl.ds(at, part), :] = values[k % 2 * part : (k % 2 + 1) * part]

    loads[0].wait()
    chosen = (iota((columns, variants), 0) == flags_ref[...]).astype(F32).astype(BF16)
    loads[1].wait()
    genotype = jnp.dot(dosage_ref[...], chosen, preferred_element_type=F32).astype(BF16)
    genotype = transposed_dot(genotype, order)
    for k in range(n):
        send[k, pl.ds(0, own), :] = genotype[k // 2 * own : (k // 2 + 1) * own]

    @pl.when(jnp.logical_and(final, spot < size // 2))
    def _():
        meet()

    @pl.when(jnp.logical_not(final))
    def _():
        pl.semaphore_wait(barrier, n - 1 - size)

    def copy(at, slot):
        return pltpu.make_async_remote_copy(
            src_ref=send.at[at], dst_ref=recv.at[slot], send_sem=send_sem.at[0], recv_sem=recv_sem.at[slot],
            device_id={"smp": at}, device_id_type=MESH,
        )

    def rcopy(at):
        return pltpu.make_async_remote_copy(
            src_ref=rsend, dst_ref=held.at[me], send_sem=rsend_sem.at[0], recv_sem=rrecv_sem.at[0],
            device_id={"smp": at}, device_id_type=MESH,
        )

    for group in reversed(range(1, planes - 1)):

        @pl.when(plane < group)
        def _():
            for at in range(size):
                copy(member(group, at), me).start()

    for at in range(1, size):
        copy(member(plane, at), me).start()

    for group in range(planes - 1):

        @pl.when(plane > group)
        def _():
            for at in range(size):
                copy(member(group, at), me).start()

    lane_e = iota((part, lanes), 1)
    lane_v = iota((own, lanes), 1)
    spread_e = (lax.div(lane_e, own) == iota((part, lanes), 0)).astype(F32)
    spread_v = jnp.logical_and(lax.rem(lane_v, own) == iota((own, lanes), 0), lane_v < own * part).astype(F32)
    none_e, none_v = jnp.zeros_like(spread_e), jnp.zeros_like(spread_v)
    spread = jnp.concatenate(
        [jnp.concatenate([none_v, none_v, spread_v], axis=1)]
        + [jnp.concatenate([spread_e, none_e, none_e], axis=1)] * 3
        + [jnp.concatenate([none_e, spread_e, none_e], axis=1)],
        axis=0,
    ).astype(BF16)

    def tile(block, t):
        return pl.ds(pl.multiple_of(block * rows + t * SUB, SUB), SUB)

    def moments(weight, dose, total, into, base):
        for k in range(4):
            total[k] = total[k] + weight
            into[base, pl.ds(k * lanes, lanes)] = total[k]
            if k < 3:
                weight = weight * dose

    zero = jnp.zeros((SUB, lanes), F32)

    def expand(slots, pieces, marked):
        mixed = []
        for values in pieces:
            doses, samples, events = values[:own], values[own : own + part], values[own + part :]
            tall = jnp.concatenate([doses, *thirds(samples), events], axis=0)
            mixed.append(transposed_dot(tall.astype(BF16), spread))
        for slot, values in zip(slots, mixed):
            total = [zero] * 4
            for t in reversed(range(steps)):
                shift, mark, dose = (values[t * SUB : (t + 1) * SUB, k * lanes : (k + 1) * lanes] for k in range(3))
                at = tile(slot, t)
                shift_ref[at, :] = shift
                mark_ref[at, :] = mark
                dose_ref[at, :] = dose
                marked = marked + mark * dose
                moments(jnp.exp2(shift), dose, total, sums_ref, at)
        return marked

    marked = expand([me], [send[me]], zero)

    @pl.when(jnp.logical_not(final))
    def _():
        pl.semaphore_wait(up.at[0], size)
        for at in range(size):
            copy(member(planes - 1, at), me).start()

    def arrive(slots, marked):
        for slot in slots:
            copy(slot, slot).wait_recv()
        return expand(slots, [recv[slot] for slot in slots], marked)

    def arrive_plane(at, marked):
        lower = lax.convert_element_type(at <= plane, jnp.int32)
        return arrive([member(lower * (plane - at) + (1 - lower) * at, to) for to in range(size)], marked)

    below = iota((SUB, lanes), 0)

    def scan(total, later):
        carry, fresh = [], []
        for x, run in zip(total, later):
            e = jnp.where(below < SUB - 1, pltpu.roll(x, SUB - 1, 0), 0.0)
            for shift in (1, 2, 4):
                e = e + jnp.where(below < SUB - shift, pltpu.roll(e, SUB - shift, 0), 0.0)
            carry.append(e + run)
            fresh.append(run + jnp.broadcast_to((x + e)[0:1], (SUB, lanes)))
        return carry, fresh

    def add_moments(block, slope, into):
        total = [zero] * 4
        for t in reversed(range(steps)):
            at = tile(block, t)
            dose = dose_ref[at, :]
            moments(jnp.exp2(shift_ref[at, :] + slope * dose), dose, total, into, pl.ds(t * SUB, SUB))
        return total

    def add_terms(block, source, base, carry, sums):
        first_sum, information, skewness = sums
        for t in reversed(range(steps)):
            here = pl.ds(base + t * SUB, SUB) if isinstance(base, int) else tile(base, t)
            s0, s1, s2, s3 = (source[here, pl.ds(k * lanes, lanes)] + carry[k] for k in range(4))
            mark = mark_ref[tile(block, t), :]
            inverse = mark * (1.0 / s0)
            one = s1 * inverse
            two = s2 * inverse
            spread = two - one * one
            first_sum = first_sum + one
            information = information + spread
            skewness = skewness + (s3 * inverse - one * (two + (spread + spread)))
        return first_sum, information, skewness

    def finish(effect, sums):
        first_sum, information, skewness = sums
        score, information, skewness = (
            jnp.sum(x, axis=0, keepdims=True) for x in (marked - first_sum, information, skewness)
        )
        effect = effect + (score + 0.5 * skewness / information) / information
        return effect, effect * jnp.sqrt(information)

    zeros = (zero,) * 3
    for k in range(7):
        state_ref[k] = zero

    def open_plane(group):
        def opening(at, state):
            block = group * size + size - 1 - at
            total = [sums_ref[tile(block, 0), pl.ds(k * lanes, lanes)] for k in range(4)]
            carry, later = scan(total, state[:4])
            return (*later, *add_terms(block, sums_ref, block, carry, state[4:]))

        state = lax.fori_loop(0, size, opening, tuple(state_ref[k] for k in range(7)), unroll=2)
        for k in range(7):
            state_ref[k] = state[k]

    marked = arrive([member(plane, at) for at in range(1, size)], marked)

    def arrive_plane(group, marked):
        return arrive([member(group, at) for at in range(size)], marked)

    marked = lax.fori_loop(plane + 1, planes, arrive_plane, marked)

    @pl.loop(plane, planes)
    def _(at):
        open_plane(planes - 1 + plane - at)

    def arrive_lower(at, marked):
        marked = arrive_plane(plane - at, marked)
        open_plane(plane - at)
        return marked

    marked = lax.fori_loop(1, plane + 1, arrive_lower, marked)
    sums = [state_ref[4 + k] for k in range(3)]
    effect, zscore = finish(jnp.zeros((1, lanes), F32), sums)

    def sweep(_, state):
        effect, _ = state
        slope = jnp.broadcast_to(effect * LOG2E, (SUB, lanes))
        carry, later = scan(add_moments(n - 1, slope, even_ref), [zero] * 4)

        def pair(at, state):
            carry, later, sums = state
            block = n - 1 - 2 * at
            total = add_moments(block - 1, slope, odd_ref)
            sums = add_terms(block, even_ref, 0, carry, sums)
            carry, later = scan(total, later)
            total = add_moments(block - 2, slope, even_ref)
            sums = add_terms(block - 1, odd_ref, 0, carry, sums)
            carry, later = scan(total, later)
            return tuple(carry), tuple(later), sums

        carry, later, sums = lax.fori_loop(0, n // 2 - 1, pair, (tuple(carry), tuple(later), zeros))
        total = add_moments(0, slope, odd_ref)
        sums = add_terms(1, even_ref, 0, carry, sums)
        carry, _ = scan(total, later)
        return finish(effect, add_terms(0, odd_ref, 0, carry, sums))

    effect, zscore = lax.fori_loop(0, ITERS - 1, sweep, (effect, zscore))

    rsend[0:1, :] = effect
    rsend[1:2, :] = zscore

    for at in range(n - 1):
        rcopy(others(at)).start()

    mine = pltpu.make_async_copy(rsend, held.at[me], load_sem.at[0])
    mine.start()
    pltpu.make_async_copy(send.at[pl.ds(0, n - 1)], recv.at[pl.ds(0, n - 1)], send_sem.at[0]).wait()
    mine.wait()
    whole = held.at[pl.ds(0, n - 1)]
    pltpu.make_async_copy(whole, whole, rrecv_sem.at[0]).wait()
    pltpu.make_async_copy(whole, whole, rsend_sem.at[0]).wait()


def unfold(n, held, effect_ref, zscore_ref):
    endpoints, variants = effect_ref.shape
    part = endpoints // 2
    own = variants * 2 // n
    lanes = held.shape[2]
    owner = lax.div(iota((part, lanes), 1), own) == iota((part, lanes), 0)
    fold = jnp.logical_and(
        lax.rem(iota((lanes, variants), 0), own) == lax.rem(iota((lanes, variants), 1), own),
        iota((lanes, variants), 0) < own * part,
    ).astype(F32).astype(BF16)
    column = lax.div(iota((endpoints, variants), 1), own)
    for which, out in enumerate((effect_ref, zscore_ref)):
        tall = jnp.concatenate([jnp.where(owner, held[k, which : which + 1, :], 0.0) for k in range(n)], axis=0)
        parts = [jnp.dot(third.astype(BF16), fold, preferred_element_type=F32) for third in thirds(tall)]
        tall = (parts[0] + parts[1]) + parts[2]
        result = jnp.zeros((endpoints, variants), F32)
        for c in range(n // 2):
            result = jnp.where(column == c, tall[c * endpoints : (c + 1) * endpoints], result)
        out[...] = result


def solution(mesh):
    n = mesh.shape["smp"]

    def body(dosage, flags, events, offsets):
        rows, columns = dosage.shape
        endpoints = offsets.shape[1]
        variants = flags.shape[0]
        own = variants * 2 // n
        part = endpoints // 2
        lanes = -(-own * part // 128) * 128
        out = jax.ShapeDtypeStruct((endpoints, variants), F32)
        held = pl.pallas_call(
            functools.partial(kernel, n),
            out_shape=jax.ShapeDtypeStruct((n, 2, lanes), F32),
            in_specs=[pl.BlockSpec(memory_space=pl.ANY)] * 4,
            out_specs=pl.BlockSpec(memory_space=pl.ANY),
            scratch_shapes=[
                pltpu.VMEM((1, variants), jnp.int32),
                pltpu.VMEM((rows, columns), BF16),
                pltpu.VMEM((endpoints, rows), F32),
                pltpu.VMEM((endpoints, rows), jnp.int32),
                pltpu.VMEM((n, own + 2 * part, rows), F32),
                pltpu.VMEM((n, own + 2 * part, rows), F32),
                pltpu.VMEM((n * rows, lanes), F32),
                pltpu.VMEM((n * rows, lanes), F32),
                pltpu.VMEM((n * rows, lanes), F32),
                pltpu.VMEM((n * rows, 4 * lanes), F32),
                pltpu.VMEM((rows, 4 * lanes), F32),
                pltpu.VMEM((rows, 4 * lanes), F32),
                pltpu.VMEM((7, SUB, lanes), F32),
                pltpu.VMEM((2, lanes), F32),
                pltpu.SemaphoreType.DMA((4,)),
                pltpu.SemaphoreType.DMA((1,)),
                pltpu.SemaphoreType.DMA((n,)),
                pltpu.SemaphoreType.DMA((1,)),
                pltpu.SemaphoreType.DMA((1,)),
                pltpu.SemaphoreType.REGULAR((1,)),
            ],
            compiler_params=pltpu.CompilerParams(collective_id=0, has_side_effects=True, vmem_limit_bytes=LIMIT),
        )(*(pltpu.with_memory_space_constraint(x, pltpu.HBM) for x in (flags.reshape(1, variants), dosage, offsets.T, events.T)))
        return pl.pallas_call(
            functools.partial(unfold, n),
            out_shape=(out, out),
            in_specs=[pl.BlockSpec(memory_space=pltpu.VMEM)],
            out_specs=[pl.BlockSpec(memory_space=pltpu.VMEM)] * 2,
            compiler_params=pltpu.CompilerParams(vmem_limit_bytes=LIMIT // 8),
        )(held)

    return jax.shard_map(
        body,
        mesh=mesh,
        in_specs=(P("smp", "grp"), P("grp"), P("smp", "grp"), P("smp", "grp")),
        out_specs=(P(None, "grp"), P(None, "grp")),
        check_vma=False,
    )
```

```python
import functools
import math

import jax
import jax.numpy as jnp
from jax import lax
from jax.experimental import pallas as pl
from jax.experimental.pallas import tpu as pltpu
from jax.sharding import PartitionSpec as P

ITERS = 3
SUB = 8
LIMIT = 48 * 2**20
LOG2E = 1.4426950408889634
MESH = pl.DeviceIdType.MESH
F32 = jnp.float32
BF16 = jnp.bfloat16


def thirds(x):
    high = x.astype(BF16).astype(F32)
    rest = x - high
    middle = rest.astype(BF16).astype(F32)
    return high, middle, rest - middle


def transposed_dot(a, b):
    return lax.dot_general(a, b, (((0,), (0,)), ((), ())), preferred_element_type=F32)


def iota(shape, dim):
    return lax.broadcasted_iota(jnp.int32, shape, dim)


def kernel(
    n, flags_hbm, dosage_hbm, offsets_hbm, events_hbm, held,
    flags_ref, dosage_ref, offsets_ref, events_ref,
    send, recv, dose_ref, shift_ref, mark_ref, sums_ref, even_ref, odd_ref, state_ref, rsend,
    load_sem, send_sem, recv_sem, rsend_sem, rrecv_sem, relay_sem, up,
):
    me = lax.axis_index("smp")
    rows, columns = dosage_ref.shape
    endpoints = offsets_ref.shape[0]
    part = endpoints // 2
    variants = flags_ref.shape[1]
    own = variants * 2 // n
    lanes = dose_ref.shape[1]
    steps = rows // SUB
    size = math.isqrt(n)
    planes = n // size
    plane, spot = lax.div(me, size), lax.rem(me, size)
    final = plane == planes - 1

    def others(at):
        return at + lax.convert_element_type(at >= me, jnp.int32)

    loads = [
        pltpu.make_async_copy(src, dst, load_sem.at[at])
        for at, (src, dst) in enumerate(
            ((flags_hbm, flags_ref), (dosage_hbm, dosage_ref), (offsets_hbm, offsets_ref), (events_hbm, events_ref))
        )
    ]
    for load in loads:
        load.start()

    barrier = pltpu.get_barrier_semaphore()

    def member(plane, at):
        return plane * size + lax.rem(spot + at, size)

    def signal(sem, at):
        pl.semaphore_signal(sem, inc=1, device_id={"smp": at}, device_id_type=MESH)

    @pl.when(final)
    def _():
        for at in range(1, size):
            signal(barrier, member(plane, at))

    @pl.when(jnp.logical_not(final))
    def _():
        for at in range(n - 1):
            signal(barrier, others(n - 2 - at))

    def meet():
        pl.semaphore_wait(barrier, n - 1)
        for at in range(n - size):
            signal(up.at[0], at)

    @pl.when(jnp.logical_and(final, spot >= size // 2))
    def _():
        meet()

    line = iota((rows, rows), 1)
    order = (iota((rows, rows), 0) == lax.rem(line, SUB) * steps + lax.div(line, SUB)).astype(F32).astype(BF16)

    loads[2].wait()
    loads[3].wait()
    four = jnp.concatenate([*thirds(offsets_ref[...] * LOG2E), events_ref[...].astype(F32)], axis=0)
    four = jnp.dot(four.astype(BF16), order, preferred_element_type=F32)
    high, middle, low_part, events = (four[k * endpoints : (k + 1) * endpoints] for k in range(4))
    offsets = (high + middle) + low_part
    for k in range(n):
        for at, values in ((0, offsets), (part, events)):
            send[k, pl.ds(at, part), :] = values[k % 2 * part : (k % 2 + 1) * part]

    loads[0].wait()
    chosen = (iota((columns, variants), 0) == flags_ref[...]).astype(F32).astype(BF16)
    loads[1].wait()
    genotype = jnp.dot(dosage_ref[...], chosen, preferred_element_type=F32).astype(BF16)
    genotype = transposed_dot(genotype, order)
    for k in range(n):
        send[k, pl.ds(2 * part, own), :] = genotype[k // 2 * own : (k // 2 + 1) * own]

    @pl.when(jnp.logical_and(final, spot < size // 2))
    def _():
        meet()

    @pl.when(jnp.logical_not(final))
    def _():
        pl.semaphore_wait(barrier, n - 1 - size)

    doses_at = pl.ds(2 * part, send.shape[1] - 2 * part)
    pair_at = pl.ds(0, 2 * part)
    side = lax.rem(me, 2)
    sibling = me + 1 - 2 * side

    def copy(at, slot):
        return pltpu.make_async_remote_copy(
            src_ref=send.at[at], dst_ref=recv.at[slot], send_sem=send_sem.at[0], recv_sem=recv_sem.at[slot],
            device_id={"smp": at}, device_id_type=MESH,
        )

    def pair_copy(at, slot):
        return pltpu.make_async_remote_copy(
            src_ref=send.at[at, pair_at], dst_ref=recv.at[slot, pair_at], send_sem=send_sem.at[1],
            recv_sem=recv_sem.at[slot], device_id={"smp": at}, device_id_type=MESH,
        )

    def relay(slot):
        return pltpu.make_async_remote_copy(
            src_ref=recv.at[slot, doses_at], dst_ref=recv.at[slot, doses_at], send_sem=send_sem.at[2],
            recv_sem=relay_sem.at[slot], device_id={"smp": sibling}, device_id_type=MESH,
        )

    def shared(group):
        return jnp.logical_and(group - plane < planes - 1, plane - group < planes - 1)

    def same(group, at):
        return group * size + 2 * lax.rem(lax.div(spot, 2) + at, size // 2) + side

    def cross(group, at):
        return group * size + 2 * lax.rem(lax.div(spot, 2) + at, size // 2) + 1 - side

    def post(group):
        for at in range(size // 2):
            copy(same(group, at), me).start()

        @pl.when(shared(group))
        def _():
            for at in range(size // 2):
                pair_copy(cross(group, at), me).start()

        @pl.when(jnp.logical_not(shared(group)))
        def _():
            for at in range(size // 2):
                copy(cross(group, at), me).start()

    def rcopy(at):
        return pltpu.make_async_remote_copy(
            src_ref=rsend, dst_ref=held.at[me], send_sem=rsend_sem.at[0], recv_sem=rrecv_sem.at[0],
            device_id={"smp": at}, device_id_type=MESH,
        )

    for group in reversed(range(1, planes - 1)):

        @pl.when(plane < group)
        def _():
            post(group)

    for at in range(1, size):
        copy(member(plane, at), me).start()

    for group in range(planes - 1):

        @pl.when(plane > group)
        def _():
            post(group)

    lane_e = iota((part, lanes), 1)
    lane_v = iota((own, lanes), 1)
    spread_e = (lax.div(lane_e, own) == iota((part, lanes), 0)).astype(F32)
    spread_v = jnp.logical_and(lax.rem(lane_v, own) == iota((own, lanes), 0), lane_v < own * part).astype(F32)
    none_e, none_v = jnp.zeros_like(spread_e), jnp.zeros_like(spread_v)
    spread = jnp.concatenate(
        [jnp.concatenate([none_v, none_v, spread_v], axis=1)]
        + [jnp.concatenate([spread_e, none_e, none_e], axis=1)] * 3
        + [jnp.concatenate([none_e, spread_e, none_e], axis=1)],
        axis=0,
    ).astype(BF16)

    def tile(block, t):
        return pl.ds(pl.multiple_of(block * rows + t * SUB, SUB), SUB)

    def moments(weight, dose, total, into, base):
        for k in range(4):
            total[k] = total[k] + weight
            into[base, pl.ds(k * lanes, lanes)] = total[k]
            if k < 3:
                weight = weight * dose

    zero = jnp.zeros((SUB, lanes), F32)

    def expand(slots, pieces, marked):
        mixed = []
        for values in pieces:
            samples, events, doses = values[:part], values[part : 2 * part], values[2 * part : 2 * part + own]
            tall = jnp.concatenate([doses, *thirds(samples), events], axis=0)
            mixed.append(transposed_dot(tall.astype(BF16), spread))
        for slot, values in zip(slots, mixed):
            total = [zero] * 4
            for t in reversed(range(steps)):
                shift, mark, dose = (values[t * SUB : (t + 1) * SUB, k * lanes : (k + 1) * lanes] for k in range(3))
                at = tile(slot, t)
                shift_ref[at, :] = shift
                mark_ref[at, :] = mark
                dose_ref[at, :] = dose
                marked = marked + mark * dose
                moments(jnp.exp2(shift), dose, total, sums_ref, at)
        return marked

    marked = expand([me], [send[me]], zero)

    @pl.when(jnp.logical_not(final))
    def _():
        pl.semaphore_wait(up.at[0], size)
        post(planes - 1)

    below = iota((SUB, lanes), 0)

    def scan(total, later):
        carry, fresh = [], []
        for x, run in zip(total, later):
            e = jnp.where(below < SUB - 1, pltpu.roll(x, SUB - 1, 0), 0.0)
            for shift in (1, 2, 4):
                e = e + jnp.where(below < SUB - shift, pltpu.roll(e, SUB - shift, 0), 0.0)
            carry.append(e + run)
            fresh.append(run + jnp.broadcast_to((x + e)[0:1], (SUB, lanes)))
        return carry, fresh

    def add_moments(block, slope, into):
        total = [zero] * 4
        for t in reversed(range(steps)):
            at = tile(block, t)
            dose = dose_ref[at, :]
            moments(jnp.exp2(shift_ref[at, :] + slope * dose), dose, total, into, pl.ds(t * SUB, SUB))
        return total

    def add_terms(block, source, base, carry, sums):
        first_sum, information, skewness = sums
        for t in reversed(range(steps)):
            here = pl.ds(base + t * SUB, SUB) if isinstance(base, int) else tile(base, t)
            s0, s1, s2, s3 = (source[here, pl.ds(k * lanes, lanes)] + carry[k] for k in range(4))
            mark = mark_ref[tile(block, t), :]
            inverse = mark * (1.0 / s0)
            one = s1 * inverse
            two = s2 * inverse
            spread = two - one * one
            first_sum = first_sum + one
            information = information + spread
            skewness = skewness + (s3 * inverse - one * (two + (spread + spread)))
        return first_sum, information, skewness

    def finish(effect, sums):
        first_sum, information, skewness = sums
        score, information, skewness = (
            jnp.sum(x, axis=0, keepdims=True) for x in (marked - first_sum, information, skewness)
        )
        effect = effect + (score + 0.5 * skewness / information) / information
        return effect, effect * jnp.sqrt(information)

    zeros = (zero,) * 3
    for k in range(7):
        state_ref[k] = zero

    def open_plane(group):
        def opening(at, state):
            block = group * size + size - 1 - at
            total = [sums_ref[tile(block, 0), pl.ds(k * lanes, lanes)] for k in range(4)]
            carry, later = scan(total, state[:4])
            return (*later, *add_terms(block, sums_ref, block, carry, state[4:]))

        state = lax.fori_loop(0, size, opening, tuple(state_ref[k] for k in range(7)), unroll=2)
        for k in range(7):
            state_ref[k] = state[k]

    own_slots = [member(plane, at) for at in range(1, size)]
    for slot in own_slots:
        copy(slot, slot).wait_recv()
    marked = expand(own_slots, [recv[slot] for slot in own_slots], marked)

    @pl.when(final)
    def _():
        open_plane(plane)

    def following(at):
        lower = lax.convert_element_type(at > planes - 1 - plane, jnp.int32)
        return lower * (planes - 1 - at) + (1 - lower) * (plane + at)

    def settle(group, marked):
        @pl.when(shared(group))
        def _():
            for at in range(size // 2):
                slot = cross(group, at)
                pair_copy(slot, slot).wait_recv()
                relay(slot).wait_recv()

        @pl.when(jnp.logical_not(shared(group)))
        def _():
            for at in range(size // 2):
                for slot in (same(group, at), cross(group, at)):
                    copy(slot, slot).wait_recv()

        slots = [member(group, at) for at in range(size)]
        marked = expand(slots, [recv[slot] for slot in slots], marked)

        @pl.when(group == planes - 1)
        def _():
            @pl.loop(plane, planes)
            def _(at):
                open_plane(planes - 1 + plane - at)

        @pl.when(group < plane)
        def _():
            open_plane(group)

        return marked

    def forward(group):
        @pl.when(shared(group))
        def _():
            for at in range(size // 2):
                slot = same(group, at)
                copy(slot, slot).wait_recv()
                relay(slot).start()

    for at in range(1, planes):
        forward(jnp.where(at > plane, at, plane - at))

    marked = lax.fori_loop(1, planes, lambda at, marked: settle(following(at), marked), marked)
    sums = [state_ref[4 + k] for k in range(3)]
    effect, zscore = finish(jnp.zeros((1, lanes), F32), sums)

    def sweep(_, state):
        effect, _ = state
        slope = jnp.broadcast_to(effect * LOG2E, (SUB, lanes))
        carry, later = scan(add_moments(n - 1, slope, even_ref), [zero] * 4)

        def pair(at, state):
            carry, later, sums = state
            block = n - 1 - 2 * at
            total = add_moments(block - 1, slope, odd_ref)
            sums = add_terms(block, even_ref, 0, carry, sums)
            carry, later = scan(total, later)
            total = add_moments(block - 2, slope, even_ref)
            sums = add_terms(block - 1, odd_ref, 0, carry, sums)
            carry, later = scan(total, later)
            return tuple(carry), tuple(later), sums

        carry, later, sums = lax.fori_loop(0, n // 2 - 1, pair, (tuple(carry), tuple(later), zeros))
        total = add_moments(0, slope, odd_ref)
        sums = add_terms(1, even_ref, 0, carry, sums)
        carry, _ = scan(total, later)
        return finish(effect, add_terms(0, odd_ref, 0, carry, sums))

    effect, zscore = lax.fori_loop(0, ITERS - 1, sweep, (effect, zscore))

    rsend[0:1, :] = effect
    rsend[1:2, :] = zscore

    for at in range(n - 1):
        rcopy(others(at)).start()

    mine = pltpu.make_async_copy(rsend, held.at[me], load_sem.at[0])
    mine.start()
    edge = jnp.logical_or(plane == 0, final)
    half = size // 2
    for here, many in ((edge, planes - 2), (jnp.logical_not(edge), planes - 1)):

        @pl.when(here)
        def _():
            full = pl.ds(0, n - 1 - many * half)
            pltpu.make_async_copy(send.at[full], recv.at[full], send_sem.at[0]).wait()
            for at, piece in ((1, pair_at), (2, doses_at)):
                part_of = pl.ds(0, many * half)
                pltpu.make_async_copy(send.at[part_of, piece], recv.at[part_of, piece], send_sem.at[at]).wait()

    mine.wait()
    whole = held.at[pl.ds(0, n - 1)]
    pltpu.make_async_copy(whole, whole, rrecv_sem.at[0]).wait()
    pltpu.make_async_copy(whole, whole, rsend_sem.at[0]).wait()


def unfold(n, held, effect_ref, zscore_ref):
    endpoints, variants = effect_ref.shape
    part = endpoints // 2
    own = variants * 2 // n
    lanes = held.shape[2]
    owner = lax.div(iota((part, lanes), 1), own) == iota((part, lanes), 0)
    fold = jnp.logical_and(
        lax.rem(iota((lanes, variants), 0), own) == lax.rem(iota((lanes, variants), 1), own),
        iota((lanes, variants), 0) < own * part,
    ).astype(F32).astype(BF16)
    column = lax.div(iota((endpoints, variants), 1), own)
    for which, out in enumerate((effect_ref, zscore_ref)):
        tall = jnp.concatenate([jnp.where(owner, held[k, which : which + 1, :], 0.0) for k in range(n)], axis=0)
        parts = [jnp.dot(third.astype(BF16), fold, preferred_element_type=F32) for third in thirds(tall)]
        tall = (parts[0] + parts[1]) + parts[2]
        result = jnp.zeros((endpoints, variants), F32)
        for c in range(n // 2):
            result = jnp.where(column == c, tall[c * endpoints : (c + 1) * endpoints], result)
        out[...] = result


def solution(mesh):
    n = mesh.shape["smp"]

    def body(dosage, flags, events, offsets):
        rows, columns = dosage.shape
        endpoints = offsets.shape[1]
        variants = flags.shape[0]
        own = variants * 2 // n
        part = endpoints // 2
        lanes = -(-own * part // 128) * 128
        held_rows = 2 * part + -(-own // SUB) * SUB
        out = jax.ShapeDtypeStruct((endpoints, variants), F32)
        held = pl.pallas_call(
            functools.partial(kernel, n),
            out_shape=jax.ShapeDtypeStruct((n, 2, lanes), F32),
            in_specs=[pl.BlockSpec(memory_space=pl.ANY)] * 4,
            out_specs=pl.BlockSpec(memory_space=pl.ANY),
            scratch_shapes=[
                pltpu.VMEM((1, variants), jnp.int32),
                pltpu.VMEM((rows, columns), BF16),
                pltpu.VMEM((endpoints, rows), F32),
                pltpu.VMEM((endpoints, rows), jnp.int32),
                pltpu.VMEM((n, held_rows, rows), F32),
                pltpu.VMEM((n, held_rows, rows), F32),
                pltpu.VMEM((n * rows, lanes), F32),
                pltpu.VMEM((n * rows, lanes), F32),
                pltpu.VMEM((n * rows, lanes), F32),
                pltpu.VMEM((n * rows, 4 * lanes), F32),
                pltpu.VMEM((rows, 4 * lanes), F32),
                pltpu.VMEM((rows, 4 * lanes), F32),
                pltpu.VMEM((7, SUB, lanes), F32),
                pltpu.VMEM((2, lanes), F32),
                pltpu.SemaphoreType.DMA((4,)),
                pltpu.SemaphoreType.DMA((3,)),
                pltpu.SemaphoreType.DMA((n,)),
                pltpu.SemaphoreType.DMA((1,)),
                pltpu.SemaphoreType.DMA((1,)),
                pltpu.SemaphoreType.DMA((n,)),
                pltpu.SemaphoreType.REGULAR((1,)),
            ],
            compiler_params=pltpu.CompilerParams(collective_id=0, has_side_effects=True, vmem_limit_bytes=LIMIT),
        )(*(pltpu.with_memory_space_constraint(x, pltpu.HBM) for x in (flags.reshape(1, variants), dosage, offsets.T, events.T)))
        return pl.pallas_call(
            functools.partial(unfold, n),
            out_shape=(out, out),
            in_specs=[pl.BlockSpec(memory_space=pltpu.VMEM)],
            out_specs=[pl.BlockSpec(memory_space=pltpu.VMEM)] * 2,
            compiler_params=pltpu.CompilerParams(vmem_limit_bytes=LIMIT // 8),
        )(held)

    return jax.shard_map(
        body,
        mesh=mesh,
        in_specs=(P("smp", "grp"), P("grp"), P("smp", "grp"), P("smp", "grp")),
        out_specs=(P(None, "grp"), P(None, "grp")),
        check_vma=False,
    )
```

```python
import functools
import math

import jax
import jax.numpy as jnp
from jax import lax
from jax.experimental import pallas as pl
from jax.experimental.pallas import tpu as pltpu
from jax.sharding import PartitionSpec as P

ITERS = 3
SUB = 8
LIMIT = 48 * 2**20
LOG2E = 1.4426950408889634
MESH = pl.DeviceIdType.MESH
F32 = jnp.float32
BF16 = jnp.bfloat16


def thirds(x):
    high = x.astype(BF16).astype(F32)
    rest = x - high
    middle = rest.astype(BF16).astype(F32)
    return high, middle, rest - middle


def transposed_dot(a, b):
    return lax.dot_general(a, b, (((0,), (0,)), ((), ())), preferred_element_type=F32)


def iota(shape, dim):
    return lax.broadcasted_iota(jnp.int32, shape, dim)


def kernel(
    n, flags_hbm, dosage_hbm, offsets_hbm, events_hbm, held,
    flags_ref, dosage_ref, offsets_ref, events_ref,
    send, recv, dose_ref, shift_ref, mark_ref, sums_ref, even_ref, odd_ref, state_ref, rsend,
    load_sem, send_sem, recv_sem, rsend_sem, rrecv_sem, relay_sem, up,
):
    me = lax.axis_index("smp")
    rows, columns = dosage_ref.shape
    endpoints = offsets_ref.shape[0]
    part = endpoints // 2
    variants = flags_ref.shape[1]
    own = variants * 2 // n
    lanes = dose_ref.shape[1]
    steps = rows // SUB
    size = math.isqrt(n)
    planes = n // size
    plane, spot = lax.div(me, size), lax.rem(me, size)
    final = plane == planes - 1

    def others(at):
        return at + lax.convert_element_type(at >= me, jnp.int32)

    loads = [
        pltpu.make_async_copy(src, dst, load_sem.at[at])
        for at, (src, dst) in enumerate(
            ((flags_hbm, flags_ref), (dosage_hbm, dosage_ref), (offsets_hbm, offsets_ref), (events_hbm, events_ref))
        )
    ]
    for load in loads:
        load.start()

    barrier = pltpu.get_barrier_semaphore()

    def member(plane, at):
        return plane * size + lax.rem(spot + at, size)

    def signal(sem, at):
        pl.semaphore_signal(sem, inc=1, device_id={"smp": at}, device_id_type=MESH)

    @pl.when(final)
    def _():
        for at in range(1, size):
            signal(barrier, member(plane, at))

    @pl.when(jnp.logical_not(final))
    def _():
        for at in range(n - 1):
            signal(barrier, others(n - 2 - at))

    def meet():
        pl.semaphore_wait(barrier, n - 1)
        for at in range(n - size):
            signal(up.at[0], at)

    @pl.when(jnp.logical_and(final, spot >= size // 2))
    def _():
        meet()

    line = iota((rows, rows), 1)
    order = (iota((rows, rows), 0) == lax.rem(line, SUB) * steps + lax.div(line, SUB)).astype(F32).astype(BF16)

    loads[2].wait()
    loads[3].wait()
    four = jnp.concatenate([*thirds(offsets_ref[...] * LOG2E), events_ref[...].astype(F32)], axis=0)
    four = jnp.dot(four.astype(BF16), order, preferred_element_type=F32)
    high, middle, low_part, events = (four[k * endpoints : (k + 1) * endpoints] for k in range(4))
    offsets = (high + middle) + low_part
    for k in range(n):
        for at, values in ((0, offsets), (part, events)):
            send[k, pl.ds(at, part), :] = values[k % 2 * part : (k % 2 + 1) * part]

    loads[0].wait()
    chosen = (iota((columns, variants), 0) == flags_ref[...]).astype(F32).astype(BF16)
    loads[1].wait()
    genotype = jnp.dot(dosage_ref[...], chosen, preferred_element_type=F32).astype(BF16)
    genotype = transposed_dot(genotype, order)
    for k in range(n):
        send[k, pl.ds(2 * part, own), :] = genotype[k // 2 * own : (k // 2 + 1) * own]

    @pl.when(jnp.logical_and(final, spot < size // 2))
    def _():
        meet()

    @pl.when(jnp.logical_not(final))
    def _():
        pl.semaphore_wait(barrier, n - 1 - size)

    doses_at = pl.ds(2 * part, send.shape[1] - 2 * part)
    pair_at = pl.ds(0, 2 * part)
    side = lax.rem(me, 2)
    sibling = me + 1 - 2 * side

    def lane_of(at, slot):
        apart = lax.convert_element_type(lax.div(at, size) != lax.div(slot, size), jnp.int32)
        return apart * lax.rem(at + slot, 2)

    def take(sem, many, piece):
        blocks = pl.ds(0, many)
        pltpu.make_async_copy(send.at[blocks, piece], recv.at[blocks, piece], sem).wait()

    every = pl.ds(0, send.shape[1])

    def copy(at, slot):
        return pltpu.make_async_remote_copy(
            src_ref=send.at[at], dst_ref=recv.at[slot], send_sem=send_sem.at[0], recv_sem=recv_sem.at[lane_of(at, slot), lax.div(slot, size)],
            device_id={"smp": at}, device_id_type=MESH,
        )

    def pair_copy(at, slot):
        return pltpu.make_async_remote_copy(
            src_ref=send.at[at, pair_at], dst_ref=recv.at[slot, pair_at], send_sem=send_sem.at[1],
            recv_sem=recv_sem.at[1, lax.div(slot, size)], device_id={"smp": at}, device_id_type=MESH,
        )

    def relay(slot):
        return pltpu.make_async_remote_copy(
            src_ref=recv.at[slot, doses_at], dst_ref=recv.at[slot, doses_at], send_sem=send_sem.at[2],
            recv_sem=relay_sem.at[lax.div(slot, size)], device_id={"smp": sibling}, device_id_type=MESH,
        )

    def shared(group):
        return jnp.logical_and(group - plane < planes - 1, plane - group < planes - 1)

    def same(group, at):
        return group * size + 2 * lax.rem(lax.div(spot, 2) + at, size // 2) + side

    def cross(group, at):
        return group * size + 2 * lax.rem(lax.div(spot, 2) + at, size // 2) + 1 - side

    def post(group):
        for at in range(size // 2):
            copy(same(group, at), me).start()

        @pl.when(shared(group))
        def _():
            for at in range(size // 2):
                pair_copy(cross(group, at), me).start()

        @pl.when(jnp.logical_not(shared(group)))
        def _():
            for at in range(size // 2):
                copy(cross(group, at), me).start()

    def rcopy(at):
        return pltpu.make_async_remote_copy(
            src_ref=rsend, dst_ref=held.at[me], send_sem=rsend_sem.at[0], recv_sem=rrecv_sem.at[0],
            device_id={"smp": at}, device_id_type=MESH,
        )

    for group in reversed(range(1, planes - 1)):

        @pl.when(plane < group)
        def _():
            post(group)

    for at in range(1, size):
        copy(member(plane, at), me).start()

    for group in range(planes - 1):

        @pl.when(plane > group)
        def _():
            post(group)

    lane_e = iota((part, lanes), 1)
    lane_v = iota((own, lanes), 1)
    spread_e = (lax.div(lane_e, own) == iota((part, lanes), 0)).astype(F32)
    spread_v = jnp.logical_and(lax.rem(lane_v, own) == iota((own, lanes), 0), lane_v < own * part).astype(F32)
    spread_e, spread_v = spread_e.astype(BF16), spread_v.astype(BF16)

    def tile(block, t):
        return pl.ds(pl.multiple_of(block * rows + t * SUB, SUB), SUB)

    def moments(weight, dose, total, into, base):
        for k in range(4):
            total[k] = weight if total[k] is None else total[k] + weight
            into[base, pl.ds(k * lanes, lanes)] = total[k]
            if k < 3:
                weight = weight * dose

    zero = jnp.zeros((SUB, lanes), F32)

    def expand(slots, pieces, marked):
        mixed = []
        for values in pieces:
            samples, events, doses = values[:part], values[part : 2 * part], values[2 * part : 2 * part + own]
            mixed.append((
                transposed_dot(jnp.concatenate(thirds(samples), axis=0).astype(BF16), jnp.concatenate([spread_e] * 3, axis=0)),
                transposed_dot(events.astype(BF16), spread_e),
                transposed_dot(doses.astype(BF16), spread_v),
            ))
        for slot, values in zip(slots, mixed):
            total = [None] * 4
            for t in reversed(range(steps)):
                shift, mark, dose = (value[t * SUB : (t + 1) * SUB] for value in values)
                at = tile(slot, t)
                shift_ref[at, :] = shift
                mark_ref[at, :] = mark
                dose_ref[at, :] = dose
                marked = marked + mark * dose
                moments(jnp.exp2(shift), dose, total, sums_ref, at)
        return marked

    marked = expand([me], [send[me]], zero)

    @pl.when(jnp.logical_not(final))
    def _():
        pl.semaphore_wait(up.at[0], size)
        post(planes - 1)

    line = iota((SUB, lanes), 0)
    kept = [(line < SUB - shift).astype(F32) for shift in (1, 1, 2, 4)]

    def scan(total, later):
        carry, fresh = [], []
        for x, run in zip(total, later):
            e = pltpu.roll(x, SUB - 1, 0) * kept[0]
            for at, shift in ((1, 1), (2, 2), (3, 4)):
                e = e + pltpu.roll(e, SUB - shift, 0) * kept[at]
            carry.append(e + run)
            fresh.append(run + jnp.broadcast_to((x + e)[0:1], (SUB, lanes)))
        return carry, fresh

    def add_moments(block, slope, into):
        total = [None] * 4
        for t in reversed(range(steps)):
            at = tile(block, t)
            dose = dose_ref[at, :]
            moments(jnp.exp2(shift_ref[at, :] + slope * dose), dose, total, into, pl.ds(t * SUB, SUB))
        return total

    def add_terms(block, source, base, carry, sums):
        first_sum, information, skewness = sums
        for t in reversed(range(steps)):
            here = pl.ds(base + t * SUB, SUB) if isinstance(base, int) else tile(base, t)
            s0, s1, s2, s3 = (source[here, pl.ds(k * lanes, lanes)] + carry[k] for k in range(4))
            mark = mark_ref[tile(block, t), :]
            inverse = mark * (1.0 / s0)
            one = s1 * inverse
            two = s2 * inverse
            spread = two - one * one
            first_sum = first_sum + one
            information = information + spread
            skewness = skewness + (s3 * inverse - one * (two + (spread + spread)))
        return first_sum, information, skewness

    def finish(effect, sums):
        first_sum, information, skewness = sums
        score, information, skewness = (
            jnp.sum(x, axis=0, keepdims=True) for x in (marked - first_sum, information, skewness)
        )
        effect = effect + (score + 0.5 * skewness / information) / information
        return effect, effect * jnp.sqrt(information)

    zeros = (zero,) * 3
    for k in range(7):
        state_ref[k] = zero

    def open_plane(group):
        def opening(at, state):
            block = group * size + size - 1 - at
            total = [sums_ref[tile(block, 0), pl.ds(k * lanes, lanes)] for k in range(4)]
            carry, later = scan(total, state[:4])
            return (*later, *add_terms(block, sums_ref, block, carry, state[4:]))

        state = lax.fori_loop(0, size, opening, tuple(state_ref[k] for k in range(7)), unroll=2)
        for k in range(7):
            state_ref[k] = state[k]

    own_slots = [member(plane, at) for at in range(1, size)]
    take(recv_sem.at[0, plane], size - 1, every)
    marked = expand(own_slots, [recv[slot] for slot in own_slots], marked)

    @pl.when(final)
    def _():
        open_plane(plane)

    def following(at):
        lower = lax.convert_element_type(at > planes - 1 - plane, jnp.int32)
        return lower * (planes - 1 - at) + (1 - lower) * (plane + at)

    def settle(group, marked):
        @pl.when(shared(group))
        def _():
            take(recv_sem.at[1, group], size // 2, pair_at)
            take(relay_sem.at[group], size // 2, doses_at)

        @pl.when(jnp.logical_not(shared(group)))
        def _():
            take(recv_sem.at[0, group], size // 2, every)
            take(recv_sem.at[1, group], size // 2, every)

        slots = [member(group, at) for at in range(size)]
        marked = expand(slots, [recv[slot] for slot in slots], marked)

        @pl.when(group == planes - 1)
        def _():
            @pl.loop(plane, planes)
            def _(at):
                open_plane(planes - 1 + plane - at)

        @pl.when(group < plane)
        def _():
            open_plane(group)

        return marked

    def forward(group):
        @pl.when(shared(group))
        def _():
            take(recv_sem.at[0, group], size // 2, every)
            for at in range(size // 2):
                relay(same(group, at)).start()

    for at in range(1, planes):
        forward(jnp.where(at > plane, at, plane - at))

    marked = lax.fori_loop(1, planes, lambda at, marked: settle(following(at), marked), marked)
    sums = [state_ref[4 + k] for k in range(3)]
    effect, zscore = finish(jnp.zeros((1, lanes), F32), sums)

    def sweep(_, state):
        effect, _ = state
        slope = jnp.broadcast_to(effect * LOG2E, (SUB, lanes))
        carry, later = scan(add_moments(n - 1, slope, even_ref), [zero] * 4)

        def pair(at, state):
            carry, later, sums = state
            block = n - 1 - 2 * at
            total = add_moments(block - 1, slope, odd_ref)
            sums = add_terms(block, even_ref, 0, carry, sums)
            carry, later = scan(total, later)
            total = add_moments(block - 2, slope, even_ref)
            sums = add_terms(block - 1, odd_ref, 0, carry, sums)
            carry, later = scan(total, later)
            return tuple(carry), tuple(later), sums

        carry, later, sums = lax.fori_loop(0, n // 2 - 1, pair, (tuple(carry), tuple(later), zeros))
        total = add_moments(0, slope, odd_ref)
        sums = add_terms(1, even_ref, 0, carry, sums)
        carry, _ = scan(total, later)
        return finish(effect, add_terms(0, odd_ref, 0, carry, sums))

    effect, zscore = lax.fori_loop(0, ITERS - 1, sweep, (effect, zscore))

    rsend[0:1, :] = effect
    rsend[1:2, :] = zscore

    for at in range(n - 1):
        rcopy(others(at)).start()

    mine = pltpu.make_async_copy(rsend, held.at[me], load_sem.at[0])
    mine.start()
    edge = jnp.logical_or(plane == 0, final)
    half = size // 2
    for here, many in ((edge, planes - 2), (jnp.logical_not(edge), planes - 1)):

        @pl.when(here)
        def _():
            full = pl.ds(0, n - 1 - many * half)
            pltpu.make_async_copy(send.at[full], recv.at[full], send_sem.at[0]).wait()
            for at, piece in ((1, pair_at), (2, doses_at)):
                part_of = pl.ds(0, many * half)
                pltpu.make_async_copy(send.at[part_of, piece], recv.at[part_of, piece], send_sem.at[at]).wait()

    mine.wait()
    whole = held.at[pl.ds(0, n - 1)]
    pltpu.make_async_copy(whole, whole, rrecv_sem.at[0]).wait()
    pltpu.make_async_copy(whole, whole, rsend_sem.at[0]).wait()


def unfold(n, held, effect_ref, zscore_ref):
    endpoints, variants = effect_ref.shape
    part = endpoints // 2
    own = variants * 2 // n
    lanes = held.shape[2]
    owner = lax.div(iota((part, lanes), 1), own) == iota((part, lanes), 0)
    fold = jnp.logical_and(
        lax.rem(iota((lanes, variants), 0), own) == lax.rem(iota((lanes, variants), 1), own),
        iota((lanes, variants), 0) < own * part,
    ).astype(F32).astype(BF16)
    column = lax.div(iota((endpoints, variants), 1), own)
    for which, out in enumerate((effect_ref, zscore_ref)):
        tall = jnp.concatenate([jnp.where(owner, held[k, which : which + 1, :], 0.0) for k in range(n)], axis=0)
        parts = [jnp.dot(third.astype(BF16), fold, preferred_element_type=F32) for third in thirds(tall)]
        tall = (parts[0] + parts[1]) + parts[2]
        result = jnp.zeros((endpoints, variants), F32)
        for c in range(n // 2):
            result = jnp.where(column == c, tall[c * endpoints : (c + 1) * endpoints], result)
        out[...] = result


def solution(mesh):
    n = mesh.shape["smp"]

    def body(dosage, flags, events, offsets):
        rows, columns = dosage.shape
        endpoints = offsets.shape[1]
        variants = flags.shape[0]
        own = variants * 2 // n
        part = endpoints // 2
        lanes = -(-own * part // 128) * 128
        held_rows = 2 * part + -(-own // SUB) * SUB
        out = jax.ShapeDtypeStruct((endpoints, variants), F32)
        held = pl.pallas_call(
            functools.partial(kernel, n),
            out_shape=jax.ShapeDtypeStruct((n, 2, lanes), F32),
            in_specs=[pl.BlockSpec(memory_space=pl.ANY)] * 4,
            out_specs=pl.BlockSpec(memory_space=pl.ANY),
            scratch_shapes=[
                pltpu.VMEM((1, variants), jnp.int32),
                pltpu.VMEM((rows, columns), BF16),
                pltpu.VMEM((endpoints, rows), F32),
                pltpu.VMEM((endpoints, rows), jnp.int32),
                pltpu.VMEM((n, held_rows, rows), F32),
                pltpu.VMEM((n, held_rows, rows), F32),
                pltpu.VMEM((n * rows, lanes), F32),
                pltpu.VMEM((n * rows, lanes), F32),
                pltpu.VMEM((n * rows, lanes), F32),
                pltpu.VMEM((n * rows, 4 * lanes), F32),
                pltpu.VMEM((rows, 4 * lanes), F32),
                pltpu.VMEM((rows, 4 * lanes), F32),
                pltpu.VMEM((7, SUB, lanes), F32),
                pltpu.VMEM((2, lanes), F32),
                pltpu.SemaphoreType.DMA((4,)),
                pltpu.SemaphoreType.DMA((3,)),
                pltpu.SemaphoreType.DMA((2, n // math.isqrt(n))),
                pltpu.SemaphoreType.DMA((1,)),
                pltpu.SemaphoreType.DMA((1,)),
                pltpu.SemaphoreType.DMA((n // math.isqrt(n),)),
                pltpu.SemaphoreType.REGULAR((1,)),
            ],
            compiler_params=pltpu.CompilerParams(collective_id=0, has_side_effects=True, vmem_limit_bytes=LIMIT),
        )(*(pltpu.with_memory_space_constraint(x, pltpu.HBM) for x in (flags.reshape(1, variants), dosage, offsets.T, events.T)))
        return pl.pallas_call(
            functools.partial(unfold, n),
            out_shape=(out, out),
            in_specs=[pl.BlockSpec(memory_space=pltpu.VMEM)],
            out_specs=[pl.BlockSpec(memory_space=pltpu.VMEM)] * 2,
            compiler_params=pltpu.CompilerParams(vmem_limit_bytes=LIMIT // 8),
        )(held)

    return jax.shard_map(
        body,
        mesh=mesh,
        in_specs=(P("smp", "grp"), P("grp"), P("smp", "grp"), P("smp", "grp")),
        out_specs=(P(None, "grp"), P(None, "grp")),
        check_vma=False,
    )
```

```python
import functools
import math

import jax
import jax.numpy as jnp
from jax import lax
from jax.experimental import pallas as pl
from jax.experimental.pallas import tpu as pltpu
from jax.sharding import PartitionSpec as P

ITERS = 3
SUB = 8
LIMIT = 48 * 2**20
LOG2E = 1.4426950408889634
MESH = pl.DeviceIdType.MESH
F32 = jnp.float32
BF16 = jnp.bfloat16


def thirds(x):
    high = x.astype(BF16).astype(F32)
    rest = x - high
    middle = rest.astype(BF16).astype(F32)
    return high, middle, rest - middle


def transposed_dot(a, b):
    return lax.dot_general(a, b, (((0,), (0,)), ((), ())), preferred_element_type=F32)


def iota(shape, dim):
    return lax.broadcasted_iota(jnp.int32, shape, dim)


def kernel(
    n, flags_hbm, dosage_hbm, offsets_hbm, events_hbm, held,
    flags_ref, dosage_ref, offsets_ref, events_ref,
    send, recv, dose_ref, shift_ref, mark_ref, sums_ref, even_ref, odd_ref, state_ref, rsend,
    load_sem, send_sem, recv_sem, rsend_sem, rrecv_sem, relay_sem, up,
):
    me = lax.axis_index("smp")
    rows, columns = dosage_ref.shape
    endpoints = offsets_ref.shape[0]
    part = endpoints // 2
    variants = flags_ref.shape[1]
    own = variants * 2 // n
    lanes = dose_ref.shape[1]
    steps = rows // SUB
    size = math.isqrt(n)
    planes = n // size
    plane, spot = lax.div(me, size), lax.rem(me, size)
    final = plane == planes - 1

    def others(at):
        return at + lax.convert_element_type(at >= me, jnp.int32)

    loads = [
        pltpu.make_async_copy(src, dst, load_sem.at[at])
        for at, (src, dst) in enumerate(
            ((flags_hbm, flags_ref), (dosage_hbm, dosage_ref), (offsets_hbm, offsets_ref), (events_hbm, events_ref))
        )
    ]
    for load in loads:
        load.start()

    barrier = pltpu.get_barrier_semaphore()

    def member(plane, at):
        return plane * size + lax.rem(spot + at, size)

    def signal(sem, at):
        pl.semaphore_signal(sem, inc=1, device_id={"smp": at}, device_id_type=MESH)

    @pl.when(final)
    def _():
        for at in range(1, size):
            signal(barrier, member(plane, at))

    @pl.when(jnp.logical_not(final))
    def _():
        for at in range(n - 1):
            signal(barrier, others(n - 2 - at))

    def meet():
        pl.semaphore_wait(barrier, n - 1)
        for at in range(n - size):
            signal(up.at[0], at)

    @pl.when(jnp.logical_and(final, spot >= size // 2))
    def _():
        meet()

    line = iota((rows, rows), 1)
    order = (iota((rows, rows), 0) == lax.rem(line, SUB) * steps + lax.div(line, SUB)).astype(F32).astype(BF16)

    loads[2].wait()
    loads[3].wait()
    four = jnp.concatenate([*thirds(offsets_ref[...] * LOG2E), events_ref[...].astype(F32)], axis=0)
    four = jnp.dot(four.astype(BF16), order, preferred_element_type=F32)
    high, middle, low_part, events = (four[k * endpoints : (k + 1) * endpoints] for k in range(4))
    offsets = (high + middle) + low_part
    for k in range(n):
        for at, values in ((0, offsets), (part, events)):
            send[k, pl.ds(at, part), :] = values[k % 2 * part : (k % 2 + 1) * part]

    loads[0].wait()
    chosen = (iota((columns, variants), 0) == flags_ref[...]).astype(F32).astype(BF16)
    loads[1].wait()
    genotype = jnp.dot(dosage_ref[...], chosen, preferred_element_type=F32).astype(BF16)
    genotype = transposed_dot(genotype, order)
    for k in range(n):
        send[k, pl.ds(2 * part, own), :] = genotype[k // 2 * own : (k // 2 + 1) * own]

    @pl.when(jnp.logical_and(final, spot < size // 2))
    def _():
        meet()

    @pl.when(jnp.logical_not(final))
    def _():
        pl.semaphore_wait(barrier, n - 1 - size)

    doses_at = pl.ds(2 * part, send.shape[1] - 2 * part)
    pair_at = pl.ds(0, 2 * part)
    side = lax.rem(me, 2)
    sibling = me + 1 - 2 * side

    def lane_of(at, slot):
        apart = lax.convert_element_type(lax.div(at, size) != lax.div(slot, size), jnp.int32)
        return apart * lax.rem(at + slot, 2)

    def take(sem, many, piece):
        blocks = pl.ds(0, many)
        pltpu.make_async_copy(send.at[blocks, piece], recv.at[blocks, piece], sem).wait()

    every = pl.ds(0, send.shape[1])

    def copy(at, slot):
        return pltpu.make_async_remote_copy(
            src_ref=send.at[at], dst_ref=recv.at[slot], send_sem=send_sem.at[0], recv_sem=recv_sem.at[lane_of(at, slot), lax.div(slot, size)],
            device_id={"smp": at}, device_id_type=MESH,
        )

    def pair_copy(at, slot):
        return pltpu.make_async_remote_copy(
            src_ref=send.at[at, pair_at], dst_ref=recv.at[slot, pair_at], send_sem=send_sem.at[1],
            recv_sem=recv_sem.at[1, lax.div(slot, size)], device_id={"smp": at}, device_id_type=MESH,
        )

    def relay(slot):
        return pltpu.make_async_remote_copy(
            src_ref=recv.at[slot, doses_at], dst_ref=recv.at[slot, doses_at], send_sem=send_sem.at[2],
            recv_sem=relay_sem.at[lax.div(slot, size)], device_id={"smp": sibling}, device_id_type=MESH,
        )

    def shared(group):
        return jnp.logical_and(group - plane < planes - 1, plane - group < planes - 1)

    def same(group, at):
        return group * size + 2 * lax.rem(lax.div(spot, 2) + at, size // 2) + side

    def cross(group, at):
        return group * size + 2 * lax.rem(lax.div(spot, 2) + at, size // 2) + 1 - side

    def post_same(group):
        for at in range(size // 2):
            copy(same(group, at), me).start()

    def post_cross(group):
        @pl.when(shared(group))
        def _():
            for at in range(size // 2):
                pair_copy(cross(group, at), me).start()

        @pl.when(jnp.logical_not(shared(group)))
        def _():
            for at in range(size // 2):
                copy(cross(group, at), me).start()

    def post(group):
        post_same(group)
        post_cross(group)

    def rcopy(at):
        return pltpu.make_async_remote_copy(
            src_ref=rsend, dst_ref=held.at[me], send_sem=rsend_sem.at[0], recv_sem=rrecv_sem.at[0],
            device_id={"smp": at}, device_id_type=MESH,
        )

    for group in reversed(range(1, planes - 1)):

        @pl.when(plane < group)
        def _():
            post(group)

    for group in range(planes - 1):

        @pl.when(plane > group)
        def _():
            post(group)

    for at in range(1, size):
        copy(member(plane, at), me).start()

    lane_e = iota((part, lanes), 1)
    lane_v = iota((own, lanes), 1)
    spread_e = (lax.div(lane_e, own) == iota((part, lanes), 0)).astype(F32)
    spread_v = jnp.logical_and(lax.rem(lane_v, own) == iota((own, lanes), 0), lane_v < own * part).astype(F32)
    spread_e, spread_v = spread_e.astype(BF16), spread_v.astype(BF16)

    def tile(block, t):
        return pl.ds(pl.multiple_of(block * rows + t * SUB, SUB), SUB)

    def moments(weight, dose, total, into, base):
        for k in range(4):
            total[k] = weight if total[k] is None else total[k] + weight
            into[base, pl.ds(k * lanes, lanes)] = total[k]
            if k < 3:
                weight = weight * dose

    zero = jnp.zeros((SUB, lanes), F32)

    def expand(slots, pieces, marked):
        mixed = []
        for values in pieces:
            samples, events, doses = values[:part], values[part : 2 * part], values[2 * part : 2 * part + own]
            mixed.append((
                transposed_dot(jnp.concatenate(thirds(samples), axis=0).astype(BF16), jnp.concatenate([spread_e] * 3, axis=0)),
                transposed_dot(events.astype(BF16), spread_e),
                transposed_dot(doses.astype(BF16), spread_v),
            ))
        for slot, values in zip(slots, mixed):
            total = [None] * 4
            for t in reversed(range(steps)):
                shift, mark, dose = (value[t * SUB : (t + 1) * SUB] for value in values)
                at = tile(slot, t)
                shift_ref[at, :] = shift
                mark_ref[at, :] = mark
                dose_ref[at, :] = dose
                marked = marked + mark * dose
                moments(jnp.exp2(shift), dose, total, sums_ref, at)
        return marked

    marked = expand([me], [send[me]], zero)

    @pl.when(jnp.logical_not(final))
    def _():
        pl.semaphore_wait(up.at[0], size)
        post(planes - 1)

    line = iota((SUB, lanes), 0)
    kept = [(line < SUB - shift).astype(F32) for shift in (1, 1, 2, 4)]

    def scan(total, later):
        carry, fresh = [], []
        for x, run in zip(total, later):
            e = pltpu.roll(x, SUB - 1, 0) * kept[0]
            for at, shift in ((1, 1), (2, 2), (3, 4)):
                e = e + pltpu.roll(e, SUB - shift, 0) * kept[at]
            carry.append(e + run)
            fresh.append(run + jnp.broadcast_to((x + e)[0:1], (SUB, lanes)))
        return carry, fresh

    def add_moments(block, slope, into):
        total = [None] * 4
        for t in reversed(range(steps)):
            at = tile(block, t)
            dose = dose_ref[at, :]
            moments(jnp.exp2(shift_ref[at, :] + slope * dose), dose, total, into, pl.ds(t * SUB, SUB))
        return total

    def add_terms(block, source, base, carry, sums):
        first_sum, information, skewness = sums
        for t in reversed(range(steps)):
            here = pl.ds(base + t * SUB, SUB) if isinstance(base, int) else tile(base, t)
            s0, s1, s2, s3 = (source[here, pl.ds(k * lanes, lanes)] + carry[k] for k in range(4))
            mark = mark_ref[tile(block, t), :]
            inverse = mark * (1.0 / s0)
            one = s1 * inverse
            two = s2 * inverse
            spread = two - one * one
            first_sum = first_sum + one
            information = information + spread
            skewness = skewness + (s3 * inverse - one * (two + (spread + spread)))
        return first_sum, information, skewness

    def finish(effect, sums):
        first_sum, information, skewness = sums
        score, information, skewness = (
            jnp.sum(x, axis=0, keepdims=True) for x in (marked - first_sum, information, skewness)
        )
        effect = effect + (score + 0.5 * skewness / information) / information
        return effect, effect * jnp.sqrt(information)

    zeros = (zero,) * 3
    for k in range(7):
        state_ref[k] = zero

    def open_plane(group):
        def opening(at, state):
            block = group * size + size - 1 - at
            total = [sums_ref[tile(block, 0), pl.ds(k * lanes, lanes)] for k in range(4)]
            carry, later = scan(total, state[:4])
            return (*later, *add_terms(block, sums_ref, block, carry, state[4:]))

        state = lax.fori_loop(0, size, opening, tuple(state_ref[k] for k in range(7)), unroll=2)
        for k in range(7):
            state_ref[k] = state[k]

    own_slots = [member(plane, at) for at in range(1, size)]
    take(recv_sem.at[0, plane], size - 1, every)
    marked = expand(own_slots, [recv[slot] for slot in own_slots], marked)

    @pl.when(final)
    def _():
        open_plane(plane)

    def following(at):
        lower = lax.convert_element_type(at > planes - 1 - plane, jnp.int32)
        return lower * (planes - 1 - at) + (1 - lower) * (plane + at)

    def settle(group, marked):
        @pl.when(shared(group))
        def _():
            take(recv_sem.at[1, group], size // 2, pair_at)
            take(relay_sem.at[group], size // 2, doses_at)

        @pl.when(jnp.logical_not(shared(group)))
        def _():
            take(recv_sem.at[0, group], size // 2, every)
            take(recv_sem.at[1, group], size // 2, every)

        slots = [member(group, at) for at in range(size)]
        marked = expand(slots, [recv[slot] for slot in slots], marked)

        @pl.when(group == planes - 1)
        def _():
            @pl.loop(plane, planes)
            def _(at):
                open_plane(planes - 1 + plane - at)

        @pl.when(group < plane)
        def _():
            open_plane(group)

        return marked

    def forward(group):
        @pl.when(shared(group))
        def _():
            take(recv_sem.at[0, group], size // 2, every)
            for at in range(size // 2):
                relay(same(group, at)).start()

    def nearest(at):
        return jnp.where(at > plane, at, plane - at)

    early = jnp.logical_and(final, side == 0)
    forward(nearest(1))
    marked = lax.cond(early, lambda marked: settle(following(1), marked), lambda marked: marked, marked)
    for at in range(2, planes):
        forward(nearest(at))

    start = 1 + lax.convert_element_type(early, jnp.int32)
    marked = lax.fori_loop(start, planes, lambda at, marked: settle(following(at), marked), marked)
    sums = [state_ref[4 + k] for k in range(3)]
    effect, zscore = finish(jnp.zeros((1, lanes), F32), sums)

    def sweep(_, state):
        effect, _ = state
        slope = jnp.broadcast_to(effect * LOG2E, (SUB, lanes))
        carry, later = scan(add_moments(n - 1, slope, even_ref), [zero] * 4)

        def pair(at, state):
            carry, later, sums = state
            block = n - 1 - 2 * at
            total = add_moments(block - 1, slope, odd_ref)
            sums = add_terms(block, even_ref, 0, carry, sums)
            carry, later = scan(total, later)
            total = add_moments(block - 2, slope, even_ref)
            sums = add_terms(block - 1, odd_ref, 0, carry, sums)
            carry, later = scan(total, later)
            return tuple(carry), tuple(later), sums

        carry, later, sums = lax.fori_loop(0, n // 2 - 1, pair, (tuple(carry), tuple(later), zeros))
        total = add_moments(0, slope, odd_ref)
        sums = add_terms(1, even_ref, 0, carry, sums)
        carry, _ = scan(total, later)
        return finish(effect, add_terms(0, odd_ref, 0, carry, sums))

    effect, zscore = lax.fori_loop(0, ITERS - 1, sweep, (effect, zscore))

    rsend[0:1, :] = effect
    rsend[1:2, :] = zscore

    for at in range(n - 1):
        rcopy(others(at)).start()

    mine = pltpu.make_async_copy(rsend, held.at[me], load_sem.at[0])
    mine.start()
    edge = jnp.logical_or(plane == 0, final)
    half = size // 2
    for here, many in ((edge, planes - 2), (jnp.logical_not(edge), planes - 1)):

        @pl.when(here)
        def _():
            full = pl.ds(0, n - 1 - many * half)
            pltpu.make_async_copy(send.at[full], recv.at[full], send_sem.at[0]).wait()
            for at, piece in ((1, pair_at), (2, doses_at)):
                part_of = pl.ds(0, many * half)
                pltpu.make_async_copy(send.at[part_of, piece], recv.at[part_of, piece], send_sem.at[at]).wait()

    mine.wait()
    whole = held.at[pl.ds(0, n - 1)]
    pltpu.make_async_copy(whole, whole, rrecv_sem.at[0]).wait()
    pltpu.make_async_copy(whole, whole, rsend_sem.at[0]).wait()


def unfold(n, held, effect_ref, zscore_ref):
    endpoints, variants = effect_ref.shape
    part = endpoints // 2
    own = variants * 2 // n
    lanes = held.shape[2]
    owner = lax.div(iota((part, lanes), 1), own) == iota((part, lanes), 0)
    fold = jnp.logical_and(
        lax.rem(iota((lanes, variants), 0), own) == lax.rem(iota((lanes, variants), 1), own),
        iota((lanes, variants), 0) < own * part,
    ).astype(F32).astype(BF16)
    column = lax.div(iota((endpoints, variants), 1), own)
    for which, out in enumerate((effect_ref, zscore_ref)):
        tall = jnp.concatenate([jnp.where(owner, held[k, which : which + 1, :], 0.0) for k in range(n)], axis=0)
        parts = [jnp.dot(third.astype(BF16), fold, preferred_element_type=F32) for third in thirds(tall)]
        tall = (parts[0] + parts[1]) + parts[2]
        result = jnp.zeros((endpoints, variants), F32)
        for c in range(n // 2):
            result = jnp.where(column == c, tall[c * endpoints : (c + 1) * endpoints], result)
        out[...] = result


def solution(mesh):
    n = mesh.shape["smp"]

    def body(dosage, flags, events, offsets):
        rows, columns = dosage.shape
        endpoints = offsets.shape[1]
        variants = flags.shape[0]
        own = variants * 2 // n
        part = endpoints // 2
        lanes = -(-own * part // 128) * 128
        held_rows = 2 * part + -(-own // SUB) * SUB
        out = jax.ShapeDtypeStruct((endpoints, variants), F32)
        held = pl.pallas_call(
            functools.partial(kernel, n),
            out_shape=jax.ShapeDtypeStruct((n, 2, lanes), F32),
            in_specs=[pl.BlockSpec(memory_space=pl.ANY)] * 4,
            out_specs=pl.BlockSpec(memory_space=pl.ANY),
            scratch_shapes=[
                pltpu.VMEM((1, variants), jnp.int32),
                pltpu.VMEM((rows, columns), BF16),
                pltpu.VMEM((endpoints, rows), F32),
                pltpu.VMEM((endpoints, rows), jnp.int32),
                pltpu.VMEM((n, held_rows, rows), F32),
                pltpu.VMEM((n, held_rows, rows), F32),
                pltpu.VMEM((n * rows, lanes), F32),
                pltpu.VMEM((n * rows, lanes), F32),
                pltpu.VMEM((n * rows, lanes), F32),
                pltpu.VMEM((n * rows, 4 * lanes), F32),
                pltpu.VMEM((rows, 4 * lanes), F32),
                pltpu.VMEM((rows, 4 * lanes), F32),
                pltpu.VMEM((7, SUB, lanes), F32),
                pltpu.VMEM((2, lanes), F32),
                pltpu.SemaphoreType.DMA((4,)),
                pltpu.SemaphoreType.DMA((3,)),
                pltpu.SemaphoreType.DMA((2, n // math.isqrt(n))),
                pltpu.SemaphoreType.DMA((1,)),
                pltpu.SemaphoreType.DMA((1,)),
                pltpu.SemaphoreType.DMA((n // math.isqrt(n),)),
                pltpu.SemaphoreType.REGULAR((1,)),
            ],
            compiler_params=pltpu.CompilerParams(collective_id=0, has_side_effects=True, vmem_limit_bytes=LIMIT),
        )(*(pltpu.with_memory_space_constraint(x, pltpu.HBM) for x in (flags.reshape(1, variants), dosage, offsets.T, events.T)))
        return pl.pallas_call(
            functools.partial(unfold, n),
            out_shape=(out, out),
            in_specs=[pl.BlockSpec(memory_space=pltpu.VMEM)],
            out_specs=[pl.BlockSpec(memory_space=pltpu.VMEM)] * 2,
            compiler_params=pltpu.CompilerParams(vmem_limit_bytes=LIMIT // 8),
        )(held)

    return jax.shard_map(
        body,
        mesh=mesh,
        in_specs=(P("smp", "grp"), P("grp"), P("smp", "grp"), P("smp", "grp")),
        out_specs=(P(None, "grp"), P(None, "grp")),
        check_vma=False,
    )
```
